256 devices in a mesh: lat: 8 (over z_lo, core), lon: 8 (over z_hi, x), chan: 4 (over y).
Axes of the slice: x: 4, y: 4, z: 8 (z_hi: 2, z_lo: 4; z = z_hi * 4 + z_lo), core: 2. Of those that a mesh axis runs over, the one named last changes fastest.
Arguments:
- queries: bfloat16 [128, 64, 2560], P('lat', 'lon', 'chan'), may hold values from -8 to 8
- keys: bfloat16 [128, 64, 2560], P('lat', 'lon', 'chan'), may hold values from -8 to 8
- values: bfloat16 [128, 64, 2560], P('lat', 'lon', 'chan'), may hold values from -6 to 6
- attn_out: bfloat16 [128, 64, 2560], P('lat', 'lon', 'chan'), may hold values from -6 to 6
- grad_out: bfloat16 [128, 64, 5120], P('lat', 'lon', 'chan'), may hold values from -6 to 6
- w_out: bfloat16 [5120, 2560], P(('lat', 'lon'), 'chan'), may hold values from -0.078125 to 0.078125
- bias_table: float32 [20, 25, 13], P('chan'), may hold values from -5 to 5
- key_mask: int32 [128, 64], replicated, may hold values 0 or 1
Outputs:
- grad_queries: bfloat16 [128, 64, 2560], P('lat', 'lon', 'chan')
- grad_keys: bfloat16 [128, 64, 2560], P('lat', 'lon', 'chan')
- grad_values: bfloat16 [128, 64, 2560], P('lat', 'lon', 'chan')
- grad_wout: float32 [5120, 2560], P(('lat', 'lon'), 'chan')
- grad_table: float32 [20, 25, 13], P('chan')
The draws below stay inside these ranges and needn't reach their ends.
All inputs are finite; a program needn't handle non-finite values.
Results may differ from the reference program's by a relative error of at most 0.007.
Values may be sent and summed in bfloat16 or wider, within the bound.
No kernel may reach another device: no remote copies, remote signals or barrier semaphores. Data moves between devices by JAX's collectives and lax.ppermute only.
A program may use at most 128 MiB of HBM per device.

```python
import jax
import jax.numpy as jnp
from jax import lax

D = 5120
HEADS = 20
HEAD_DIM = 128
WIN = 13
LAT_ALL = 128
LON_ALL = 64


def draw_pair(key):
    dims_all = (LAT_ALL, LON_ALL, HEADS * HEAD_DIM)
    query_draw = jnp.clip(jax.random.normal(jax.random.fold_in(key, 21), dims_all, jnp.float32), -6.0, 6.0)
    key_draw = jnp.clip(jax.random.normal(jax.random.fold_in(key, 22), dims_all, jnp.float32), -6.0, 6.0)
    return (query_draw, key_draw)


def draw_queries(key, part):
    return draw_pair(key)[0].astype(jnp.bfloat16)


def draw_keys(key, part):
    return draw_pair(key)[1].astype(jnp.bfloat16)


def plant(drawn, own_key, least, top_value):
    place = [jax.random.randint(jax.random.fold_in(own_key, axis), (), 0, length) for axis, length in enumerate(drawn.shape)]
    main_axis = drawn.shape.index(max(drawn.shape))
    neighbour = place[:main_axis] + [(place[main_axis] + 1) % drawn.shape[main_axis]] + place[main_axis + 1:]
    return drawn.at[tuple(place)].set(least).at[tuple(neighbour)].set(top_value)


def steps_of(own_key, extent, pieces, smallest, high):
    factor_of, own = 1.0, jax.random.fold_in(own_key, 6)
    for position, parts in pieces:
        steps = jnp.exp(jax.random.uniform(jax.random.fold_in(own, position), (parts,), jnp.float32, smallest / len(pieces), high / len(pieces)))
        factor_of = factor_of * jnp.repeat(steps, extent[position] // parts).reshape([-1 if axis == position else 1 for axis in range(len(extent))])
    return factor_of


def noise(rng, dims, spread, most, split=(), held_as=jnp.bfloat16):
    factor_of = steps_of(rng, dims, split, -0.22, 0.18) if split else 1.0
    entries = jax.random.normal(rng, dims, jnp.float32) * spread * factor_of
    return jnp.minimum(jnp.maximum(entries, -most), most).astype(held_as)


def setup_inputs(seed: int = 0) -> dict:
    splits = jax.random.split(jax.random.key(seed), 9)
    return {
        "queries": draw_queries(jax.random.fold_in(splits[8], 71), 0),
        "keys": draw_keys(jax.random.fold_in(splits[8], 71), 0),
        "values": noise(splits[2], (LAT_ALL, LON_ALL, HEADS * HEAD_DIM), 1.0, 6.0, ((0, 8), (1, 8), (2, 4))),
        "attn_out": noise(splits[3], (LAT_ALL, LON_ALL, HEADS * HEAD_DIM), 1.0, 6.0, ((0, 8), (1, 8), (2, 4))),
        "grad_out": noise(splits[4], (LAT_ALL, LON_ALL, D), 1.0, 6.0, ((0, 8), (1, 8), (2, 4))),
        "w_out": noise(splits[5], (D, HEADS * HEAD_DIM), D ** -0.5, 0.078125, ((0, 64), (1, 4))),
        "bias_table": noise(splits[6], (HEADS, 2 * WIN - 1, WIN), 1.0, 5.0, ((0, 4),), jnp.float32),
        "key_mask": plant((jax.random.randint(splits[7], (LAT_ALL, LON_ALL), 0, 4) < 3).astype(jnp.int32), jax.random.fold_in(splits[7], 1), 0, 1),
    }


def reference(queries, keys, values, attn_out, grad_out, w_out, bias_table, key_mask):
    lat_total, lon_total, chan_width = queries.shape
    head_count = bias_table.shape[0]
    reach_cells = WIN // 2
    score_scale = HEAD_DIM ** -0.5
    token_count = lat_total * lon_total
    flat_grad = grad_out.reshape(token_count, -1)
    grad_attn = jnp.dot(flat_grad, w_out, preferred_element_type=jnp.float32).astype(jnp.bfloat16)
    grad_attn = grad_attn.reshape(lat_total, lon_total, head_count, HEAD_DIM)
    grad_wout = lax.dot_general(flat_grad, attn_out.reshape(token_count, chan_width), (((0,), (0,)), ((), ())), preferred_element_type=jnp.float32)
    lat_index = jnp.arange(lat_total, dtype=jnp.int32)
    lon_index = jnp.arange(lon_total, dtype=jnp.int32)
    valid_keys = (key_mask == 1) | ((lat_index % 4 == 0)[:, None] & (lon_index % 4 == 0)[None, :])
    pick_cols = ((lon_index[:, None] + jnp.arange(WIN, dtype=jnp.int32)[None, :] - reach_cells) % lon_total).astype(jnp.int32)
    query_heads = queries.reshape(lat_total, lon_total, head_count, HEAD_DIM)
    key_heads = keys.reshape(lat_total, lon_total, head_count, HEAD_DIM)
    value_heads = values.reshape(lat_total, lon_total, head_count, HEAD_DIM)

    def row_step(state_sum, row_index):
        grad_k, grad_v, grad_tab = state_sum
        first_row = jnp.clip(row_index - reach_cells, 0, lat_total - WIN).astype(jnp.int32)
        key_rows = lax.dynamic_slice_in_dim(key_heads, first_row, WIN, 0).astype(jnp.float32)
        value_rows = lax.dynamic_slice_in_dim(value_heads, first_row, WIN, 0).astype(jnp.float32)
        key_pick = key_rows[:, pick_cols]
        value_pick = value_rows[:, pick_cols]
        query_h = lax.dynamic_index_in_dim(query_heads, row_index, 0, keepdims=False).astype(jnp.float32)
        grad_row = lax.dynamic_index_in_dim(grad_attn, row_index, 0, keepdims=False).astype(jnp.float32)
        key_ok = lax.dynamic_slice_in_dim(valid_keys, first_row, WIN, 0)[:, pick_cols]
        allowed = key_ok.transpose(1, 0, 2)
        table_first = (first_row - row_index + WIN - 1).astype(jnp.int32)
        table_rows = lax.dynamic_slice_in_dim(bias_table, table_first, WIN, 1)
        scores = score_scale * jnp.einsum('chd,xckhd->hcxk', query_h, key_pick) + table_rows[:, None]
        scores = jnp.where(allowed[None], scores, -1e30)
        row_max = jnp.max(scores, axis=(2, 3), keepdims=True)
        weights_exp = jnp.exp(scores - row_max)
        prob_rows = weights_exp / jnp.sum(weights_exp, axis=(2, 3), keepdims=True)
        grad_prob = jnp.einsum('chd,xckhd->hcxk', grad_row, value_pick)
        row_delta = jnp.sum(prob_rows * grad_prob, axis=(2, 3), keepdims=True)
        dscore = prob_rows * (grad_prob - row_delta)
        table_part = jnp.sum(dscore, axis=1)
        prior_sum = lax.dynamic_slice_in_dim(grad_tab, table_first, WIN, 1)
        grad_tab = lax.dynamic_update_slice_in_dim(grad_tab, prior_sum + table_part, table_first, 1)
        dscore_low = lax.optimization_barrier(dscore.astype(jnp.bfloat16)).astype(jnp.float32)
        prob_low = lax.optimization_barrier(prob_rows.astype(jnp.bfloat16)).astype(jnp.float32)
        grad_query = (score_scale * jnp.einsum('hcxk,xckhd->chd', dscore_low, key_pick)).astype(jnp.bfloat16)
        key_part = score_scale * jnp.einsum('hcxk,chd->xckhd', dscore_low, query_h)
        value_part = jnp.einsum('hcxk,chd->xckhd', prob_low, grad_row)
        zero_rows = jnp.zeros((WIN, lon_total, head_count, HEAD_DIM), jnp.float32)
        key_add = zero_rows.at[:, pick_cols].add(key_part)
        value_add = zero_rows.at[:, pick_cols].add(value_part)
        prior_k = lax.dynamic_slice_in_dim(grad_k, first_row, WIN, 0)
        grad_k = lax.dynamic_update_slice_in_dim(grad_k, prior_k + key_add, first_row, 0)
        prior_v = lax.dynamic_slice_in_dim(grad_v, first_row, WIN, 0)
        grad_v = lax.dynamic_update_slice_in_dim(grad_v, prior_v + value_add, first_row, 0)
        return (grad_k, grad_v, grad_tab), grad_query

    zero_field = jnp.zeros((lat_total, lon_total, head_count, HEAD_DIM), jnp.float32)
    start_state = (zero_field, zero_field, jnp.zeros((head_count, 2 * WIN - 1, WIN), jnp.float32))
    (sum_k, sum_v, grad_table), grad_rows = lax.scan(row_step, start_state, lat_index)
    grad_queries = grad_rows.reshape(lat_total, lon_total, chan_width)
    grad_keys = sum_k.astype(jnp.bfloat16).reshape(lat_total, lon_total, chan_width)
    grad_values = sum_v.astype(jnp.bfloat16).reshape(lat_total, lon_total, chan_width)
    return (grad_queries, grad_keys, grad_values, grad_wout, grad_table)
```

```python
import jax
import jax.numpy as jnp
from jax import lax
from jax.experimental import pallas as pl
from jax.experimental.pallas import tpu as pltpu
from jax.sharding import PartitionSpec as P

HEAD_DIM = 128
WIN = 13
REACH = 6
NEG = -1e30
F32 = jnp.float32
BF16 = jnp.bfloat16
SEG_ROWS = 32
ROWS = 16
COLS = 8
EXT_ROWS = ROWS + 2 * REACH
SEG = SEG_ROWS * COLS
USED = EXT_ROWS * COLS
SHIFTED = (SEG_ROWS + ROWS) * COLS


def dot_t0(a, b):
    return lax.dot_general(a, b, (((0,), (0,)), ((), ())), preferred_element_type=F32)


def dot_t1(a, b):
    return lax.dot_general(a, b, (((1,), (1,)), ((), ())), preferred_element_type=F32)


def grad_attn_body(grad_ref, w_ref, out_ref):
    total = dot_t0(grad_ref[0, 0], w_ref[0])
    for c in range(1, grad_ref.shape[0]):
        total = total + dot_t0(grad_ref[c, 0], w_ref[c])
    out_ref[0] = total.astype(BF16)


def grad_attn_parts(grad_feats, w_rows):
    chans, groups, feats, tokens = grad_feats.shape
    width = w_rows.shape[2]
    return pl.pallas_call(
        grad_attn_body,
        grid=(groups,),
        in_specs=[
            pl.BlockSpec((chans, 1, feats, tokens), lambda i: (0, i, 0, 0)),
            pl.BlockSpec((chans, feats, width), lambda i: (0, 0, 0)),
        ],
        out_specs=pl.BlockSpec((1, tokens, width), lambda i: (i, 0, 0)),
        out_shape=jax.ShapeDtypeStruct((groups, tokens, width), BF16),
        name="grad_attn_parts",
    )(grad_feats, w_rows)


def grad_wout_body(grad_ref, attn_ref, out_ref):
    first = pl.program_id(0) == 0
    for c in range(grad_ref.shape[0]):
        part = jnp.dot(grad_ref[c, 0], attn_ref[0], preferred_element_type=F32)

        @pl.when(first)
        def _():
            out_ref[c] = part

        @pl.when(jnp.logical_not(first))
        def _():
            out_ref[c] = out_ref[c] + part


def grad_wout_part(grad_feats, attn_rows):
    chans, groups, feats, tokens = grad_feats.shape
    width = attn_rows.shape[2]
    return pl.pallas_call(
        grad_wout_body,
        grid=(groups,),
        in_specs=[
            pl.BlockSpec((chans, 1, feats, tokens), lambda i: (0, i, 0, 0)),
            pl.BlockSpec((1, tokens, width), lambda i: (i, 0, 0)),
        ],
        out_specs=pl.BlockSpec((chans, feats, width), lambda i: (0, 0, 0)),
        out_shape=jax.ShapeDtypeStruct((chans, feats, width), F32),
        name="grad_wout_part",
    )(grad_feats, attn_rows)


def attn_body(q_ref, part_ref, left_ref, core_ref, right_ref, bias_ref, mask_ref,
              dq_ref, dleft_ref, dcore_ref, dright_ref, table_ref, bias_all):
    scale = HEAD_DIM ** (-0.5)
    tokens = ROWS * COLS
    for i in range(ROWS):
        off = (ROWS - 1 - i) * COLS
        for s in range(3):
            row = bias_ref[0, s]
            if off:
                row = pltpu.roll(row, SHIFTED - off, 1)
            row = row[:, :SEG] + mask_ref[i : i + 1, s * SEG : (s + 1) * SEG]
            bias_all[i * COLS : (i + 1) * COLS, s * SEG : (s + 1) * SEG] = row
    q = q_ref[...]
    do_sum = part_ref[0].astype(F32)
    for g in range(1, part_ref.shape[0]):
        do_sum = do_sum + part_ref[g].astype(F32)
    do = do_sum.astype(BF16)
    fill = jnp.zeros((SEG - USED, HEAD_DIM), BF16)
    k = jnp.concatenate([left_ref[0], fill, core_ref[0], fill, right_ref[0], fill], axis=0)
    v = jnp.concatenate([left_ref[1], fill, core_ref[1], fill, right_ref[1], fill], axis=0)
    scores = dot_t1(q, k) * scale + bias_all[...]
    row_max = jnp.max(scores, axis=1, keepdims=True)
    weights = jnp.exp(scores - row_max)
    probs = weights * (1.0 / jnp.sum(weights, axis=1, keepdims=True))
    grad_probs = dot_t1(do, v)
    delta = jnp.sum(probs * grad_probs, axis=1, keepdims=True)
    dscore = probs * (grad_probs - delta)
    dscore_low = dscore.astype(BF16)
    prob_low = probs.astype(BF16)
    dq_ref[...] = (scale * jnp.dot(dscore_low, k, preferred_element_type=F32)).astype(BF16)
    dk = scale * dot_t0(dscore_low, q)
    dv = dot_t0(prob_low, do)
    for n, part in enumerate((dk, dv)):
        dleft_ref[n] = part[:USED].astype(BF16)
        dcore_ref[n] = part[SEG : SEG + USED]
        dright_ref[n] = part[2 * SEG : 2 * SEG + USED].astype(BF16)
    bias_all[...] = dscore
    tail = jnp.zeros((COLS, SHIFTED - SEG), F32)
    for s in range(3):
        acc = None
        for i in range(ROWS):
            off = (ROWS - 1 - i) * COLS
            piece = bias_all[i * COLS : (i + 1) * COLS, s * SEG : (s + 1) * SEG]
            piece = jnp.concatenate([piece, tail], axis=1)
            if off:
                piece = pltpu.roll(piece, off, 1)
            acc = piece if acc is None else acc + piece
        table_ref[0, s] = acc


def attn_backward(queries, parts, left, core, right, bias_rows, mask):
    tokens, width = queries.shape
    heads = width // HEAD_DIM
    groups = parts.shape[0]
    seg_in = pl.BlockSpec((2, USED, HEAD_DIM), lambda h: (0, 0, h))
    seg_low = jax.ShapeDtypeStruct((2, USED, width), BF16)
    return pl.pallas_call(
        attn_body,
        grid=(heads,),
        in_specs=[
            pl.BlockSpec((tokens, HEAD_DIM), lambda h: (0, h)),
            pl.BlockSpec((groups, tokens, HEAD_DIM), lambda h: (0, 0, h)),
            seg_in,
            seg_in,
            seg_in,
            pl.BlockSpec((1, 3, COLS, SHIFTED), lambda h: (h, 0, 0, 0)),
            pl.BlockSpec((ROWS, 3 * SEG), lambda h: (0, 0)),
        ],
        out_specs=[
            pl.BlockSpec((tokens, HEAD_DIM), lambda h: (0, h)),
            seg_in,
            seg_in,
            seg_in,
            pl.BlockSpec((1, 3, COLS, SHIFTED), lambda h: (h, 0, 0, 0)),
        ],
        out_shape=[
            jax.ShapeDtypeStruct((tokens, width), BF16),
            seg_low,
            jax.ShapeDtypeStruct((2, USED, width), F32),
            seg_low,
            jax.ShapeDtypeStruct((heads, 3, COLS, SHIFTED), F32),
        ],
        scratch_shapes=[pltpu.VMEM((tokens, 3 * SEG), F32)],
        name="attn_backward",
    )(queries, parts, left, core, right, bias_rows, mask)


def shift(value, axis, step, wrap):
    count = lax.axis_size(axis)
    pairs = [
        (i, (i + step) % count) for i in range(count) if wrap or 0 <= i + step < count
    ]
    return lax.ppermute(value, axis, pairs)


def make_mask(key_mask):
    lat_total, lon_total = key_mask.shape
    lat, lon = lax.axis_index("lat"), lax.axis_index("lon")
    rows = lax.broadcasted_iota(jnp.int32, key_mask.shape, 0)
    cols = lax.broadcasted_iota(jnp.int32, key_mask.shape, 1)
    valid = ((key_mask == 1) | ((rows % 4 == 0) & (cols % 4 == 0))).astype(F32)
    valid = jnp.pad(valid, ((REACH, SEG_ROWS - ROWS - REACH), (0, 0)))
    valid = jnp.concatenate([valid[:, -COLS:], valid, valid[:, :COLS]], axis=1)
    valid = lax.dynamic_slice(valid, (lat * ROWS, lon * COLS), (SEG_ROWS, 3 * COLS))
    valid = valid.reshape(SEG_ROWS, 3, COLS).transpose(1, 0, 2).reshape(1, 3 * SEG)
    row_of = (lax.broadcasted_iota(jnp.int32, (ROWS, 3 * SEG), 1) // COLS) % SEG_ROWS
    query = lat * ROWS + lax.broadcasted_iota(jnp.int32, (ROWS, 3 * SEG), 0)
    low = jnp.clip(query - REACH, 0, lat_total - WIN) - lat * ROWS + REACH
    allowed = (row_of >= low) & (row_of < low + WIN) & (valid > 0)
    return jnp.where(allowed, 0.0, NEG).astype(F32)


def spread_bias(table):
    heads, offsets, _ = table.shape
    pad_y = COLS + 1
    padded = jnp.pad(
        table,
        ((0, 0), (ROWS - 1 - REACH, SEG_ROWS + ROWS - offsets - (ROWS - 1 - REACH)), (pad_y, pad_y)),
        constant_values=NEG,
    )
    pieces = []
    for s in range(3):
        for j in range(COLS):
            first = COLS * (s - 1) - j + REACH + pad_y
            pieces.append(padded[:, :, first : first + COLS])
    return jnp.stack(pieces, axis=1).reshape(heads, 3, COLS, SHIFTED)


def gather_table(spread):
    heads = spread.shape[0]
    offsets = 2 * WIN - 1
    first_row = ROWS - 1 - REACH
    grid = spread.reshape(heads, 3, COLS, SEG_ROWS + ROWS, COLS)[:, :, :, first_row : first_row + offsets]
    pad_y = COLS + 1
    total = jnp.zeros((heads, offsets, WIN + 2 * pad_y), F32)
    for s in range(3):
        for j in range(COLS):
            first = COLS * (s - 1) - j + REACH + pad_y
            total = total + jnp.pad(
                grid[:, s, j], ((0, 0), (0, 0), (first, WIN + 2 * pad_y - COLS - first))
            )
    return total[:, :, pad_y : pad_y + WIN]


def local(queries, keys, values, attn_out, grad_out, w_out, bias_table, key_mask):
    lat_rows, lon_cols, width = queries.shape
    tokens = lat_rows * lon_cols
    feats_local = grad_out.shape[2]
    lon_n = lax.axis_size("lon")
    lat_n = lax.axis_size("lat")
    chan_n = lax.axis_size("chan")
    w_rows_local = w_out.shape[0]
    per_chan = feats_local // (lon_n * w_rows_local)

    kv = jnp.stack([keys, values])
    above = shift(kv[:, lat_rows - REACH :], "lat", 1, False)
    below = shift(kv[:, :REACH], "lat", -1, False)

    grad_t = grad_out.reshape(tokens, feats_local).T
    grad_t = grad_t.reshape(per_chan, lon_n, w_rows_local, tokens).transpose(1, 0, 2, 3)
    grad_t = grad_t.reshape(lon_n, per_chan * w_rows_local, tokens)
    grad_x = lax.all_to_all(grad_t, "lon", 0, 0)
    grad_feats = lax.all_to_all(
        jnp.broadcast_to(grad_x[None], (chan_n, *grad_x.shape)), "chan", 0, 0
    )
    w_rows = lax.all_gather(w_out, "lat", axis=0).reshape(
        chan_n, per_chan * w_rows_local, width
    )
    attn_rows = lax.all_gather(attn_out.reshape(tokens, width), "lon", axis=0)

    core = jnp.concatenate([above, kv, below], axis=1).reshape(2, USED, width)
    left = shift(core, "lon", 1, True)
    right = shift(core, "lon", -1, True)

    parts = lax.all_to_all(grad_attn_parts(grad_feats, w_rows), "lon", 0, 0)

    wout_part = grad_wout_part(grad_feats, attn_rows).reshape(lat_n * w_rows_local, width)
    grad_wout = lax.psum_scatter(wout_part, "lat", scatter_dimension=0, tiled=True)

    dq, dleft, dcore, dright, spread = attn_backward(
        queries.reshape(tokens, width),
        parts,
        left,
        core,
        right,
        spread_bias(bias_table),
        make_mask(key_mask),
    )
    from_right = shift(dleft, "lon", -1, True)
    from_left = shift(dright, "lon", 1, True)
    table = gather_table(spread)
    table = jnp.pad(table.reshape(-1), (0, -table.size % 1024)).reshape(-1, 128)
    table = jnp.sum(lax.all_to_all(jnp.broadcast_to(table[None], (lat_n, *table.shape)), "lat", 0, 0), axis=0)
    folded = dcore + from_right.astype(F32) + from_left.astype(F32)
    edge = REACH * COLS
    from_below = shift(folded[:, :edge].astype(BF16), "lat", -1, False)
    from_above = shift(folded[:, USED - edge :].astype(BF16), "lat", 1, False)
    table = jnp.sum(lax.all_to_all(jnp.broadcast_to(table[None], (lon_n, *table.shape)), "lon", 0, 0), axis=0)
    grad_table = table.reshape(-1)[: bias_table.size].reshape(bias_table.shape)
    folded = folded[:, edge : USED - edge]
    folded = folded + jnp.pad(from_above.astype(F32), ((0, 0), (0, tokens - edge), (0, 0)))
    folded = folded + jnp.pad(from_below.astype(F32), ((0, 0), (tokens - edge, 0), (0, 0)))
    folded = folded.astype(BF16).reshape(2, lat_rows, lon_cols, width)
    return (
        dq.reshape(lat_rows, lon_cols, width),
        folded[0],
        folded[1],
        grad_wout,
        grad_table,
    )


def solution(mesh):
    return jax.shard_map(
        local,
        mesh=mesh,
        in_specs=(
            P("lat", "lon", "chan"),
            P("lat", "lon", "chan"),
            P("lat", "lon", "chan"),
            P("lat", "lon", "chan"),
            P("lat", "lon", "chan"),
            P(("lat", "lon"), "chan"),
            P("chan", None, None),
            P(),
        ),
        out_specs=(
            P("lat", "lon", "chan"),
            P("lat", "lon", "chan"),
            P("lat", "lon", "chan"),
            P(("lat", "lon"), "chan"),
            P("chan", None, None),
        ),
        check_vma=False,
    )
```

```python
import jax
import jax.numpy as jnp
from jax import lax
from jax.experimental import pallas as pl
from jax.experimental.pallas import tpu as pltpu
from jax.sharding import PartitionSpec as P

HEAD_DIM = 128
WIN = 13
LON = ("zh", "x")
LAT = ("zl", "core")
RING = ("zh", "zl")
REACH = 6
NEG = -1e30
F32 = jnp.float32
BF16 = jnp.bfloat16
SEG_ROWS = 32
ROWS = 16
COLS = 8
EXT_ROWS = ROWS + 2 * REACH
SEG = SEG_ROWS * COLS
USED = EXT_ROWS * COLS
EDGE = REACH * COLS
SHIFTED = (SEG_ROWS + ROWS) * COLS


def dot_t0(a, b):
    return lax.dot_general(a, b, (((0,), (0,)), ((), ())), preferred_element_type=F32)


def dot_t1(a, b):
    return lax.dot_general(a, b, (((1,), (1,)), ((), ())), preferred_element_type=F32)


def grad_attn_body(core_ref, grad_ref, own_ref, other_ref, out_ref):
    core = core_ref[0]
    chans, rows = grad_ref.shape[1], grad_ref.shape[3] // 2
    total = None
    for w_ref, pick in ((own_ref, core), (other_ref, 1 - core)):
        grads = [grad_ref[0, c, pick] for c in range(chans)]
        grads = jnp.concatenate(
            [g[z * rows : (z + 1) * rows] for z in range(2) for g in grads], axis=0
        )
        part = dot_t0(grads, w_ref[...])
        total = part if total is None else total + part
    out_ref[0] = total.astype(BF16)


def grad_attn_parts(grad_feats, w_own, w_other, core):
    groups, chans, cores, feats, tokens = grad_feats.shape
    width = w_own.shape[1]
    w_spec = pl.BlockSpec(w_own.shape, lambda i, _: (0, 0))
    return pl.pallas_call(
        grad_attn_body,
        grid_spec=pltpu.PrefetchScalarGridSpec(
            num_scalar_prefetch=1,
            grid=(groups,),
            in_specs=[
                pl.BlockSpec((1, chans, cores, feats, tokens), lambda i, _: (i, 0, 0, 0, 0)),
                w_spec,
                w_spec,
            ],
            out_specs=pl.BlockSpec((1, tokens, width), lambda i, _: (i, 0, 0)),
        ),
        out_shape=jax.ShapeDtypeStruct((groups, tokens, width), BF16),
        name="grad_attn_parts",
    )(core, grad_feats, w_own, w_other)


def grad_wout_body(place_ref, grad_ref, *refs):
    attn_refs, (mine_ref, other_ref) = refs[:-2], refs[-2:]
    groups = grad_ref.shape[0]
    core, x = place_ref[0], place_ref[1]
    attn = jnp.concatenate([ref[...] for ref in attn_refs], axis=0)
    for out_ref, pick in ((mine_ref, core), (other_ref, 1 - core)):
        grads = jnp.concatenate(
            [grad_ref[(x + groups - r) % groups, 0, pick] for r in range(groups)], axis=1
        )
        part = jnp.dot(grads, attn, preferred_element_type=F32)
        rows = out_ref.shape[2]
        for z in range(2):
            out_ref[z, 0] = part[z * rows : (z + 1) * rows].astype(out_ref.dtype)


def grad_wout_parts(grad_feats, attn_rows, place):
    groups, chans, cores, feats, tokens = grad_feats.shape
    width = attn_rows[0].shape[1]
    out_spec = pl.BlockSpec((2, 1, feats // 2, width), lambda c, _: (0, c, 0, 0))
    attn_spec = pl.BlockSpec((tokens, width), lambda c, _: (0, 0))
    return pl.pallas_call(
        grad_wout_body,
        grid_spec=pltpu.PrefetchScalarGridSpec(
            num_scalar_prefetch=1,
            grid=(chans,),
            in_specs=[
                pl.BlockSpec((groups, 1, cores, feats, tokens), lambda c, _: (0, c, 0, 0, 0)),
            ]
            + [attn_spec] * groups,
            out_specs=[out_spec, out_spec],
        ),
        out_shape=[
            jax.ShapeDtypeStruct((2, chans, feats // 2, width), F32),
            jax.ShapeDtypeStruct((2, chans, feats // 2, width), BF16),
        ],
        name="grad_wout_parts",
    )(place, grad_feats, *attn_rows)


def spread_rows(halves):
    shape = (COLS, SHIFTED)
    low = jnp.broadcast_to(halves[0:1], shape)
    high = jnp.broadcast_to(halves[1:2], shape)
    lane = lax.broadcasted_iota(jnp.int32, shape, 1) % COLS
    rel = lane - lax.broadcasted_iota(jnp.int32, shape, 0) - (COLS - REACH)

    def turn(value, first):
        if first < 0:
            value = pltpu.roll(value, first % SHIFTED, 1)
        return pltpu.roll(value, max(first, 0), 1, stride=1, stride_axis=0)

    skip = COLS - REACH
    none = jnp.full(shape, NEG, F32)
    return (
        jnp.where(rel >= 0, turn(low, skip), none),
        jnp.where(rel >= 0, turn(high, skip), jnp.where(rel >= -COLS, turn(low, skip - COLS), none)),
        jnp.where(
            rel >= 0,
            none,
            jnp.where(rel >= -COLS, turn(high, skip - COLS), turn(low, skip - 2 * COLS)),
        ),
    )


def attn_body(q_ref, part_ref, above_ref, mid_ref, below_ref, bias_ref, mask_ref,
              dq_ref, dabove_ref, dmid_ref, dbelow_ref, table_ref, bias_all):
    scale = HEAD_DIM ** (-0.5)
    tokens = ROWS * COLS
    spread = spread_rows(bias_ref[0])
    for i in range(ROWS):
        off = (ROWS - 1 - i) * COLS
        for s in range(3):
            row = spread[s]
            if off:
                row = pltpu.roll(row, SHIFTED - off, 1)
            row = row[:, :SEG] + mask_ref[i : i + 1, s * SEG : (s + 1) * SEG]
            bias_all[i * COLS : (i + 1) * COLS, s * SEG : (s + 1) * SEG] = row
    q = q_ref[...]
    do_sum = part_ref[0].astype(F32)
    for g in range(1, part_ref.shape[0]):
        do_sum = do_sum + part_ref[g].astype(F32)
    do = do_sum.astype(BF16)
    fill = jnp.zeros((SEG - USED, HEAD_DIM), BF16)
    k, v = (
        jnp.concatenate(
            [
                piece
                for s in range(3)
                for piece in (above_ref[n, s], mid_ref[n, s], below_ref[n, s], fill)
            ],
            axis=0,
        )
        for n in range(2)
    )
    scores = dot_t1(q, k) * scale + bias_all[...]
    row_max = jnp.max(scores, axis=1, keepdims=True)
    weights = jnp.exp(scores - row_max)
    probs = weights * (1.0 / jnp.sum(weights, axis=1, keepdims=True))
    grad_probs = dot_t1(do, v)
    delta = jnp.sum(probs * grad_probs, axis=1, keepdims=True)
    dscore = probs * (grad_probs - delta)
    dscore_low = dscore.astype(BF16)
    prob_low = probs.astype(BF16)
    dq_ref[...] = (scale * jnp.dot(dscore_low, k, preferred_element_type=F32)).astype(BF16)
    dk = scale * dot_t0(dscore_low, q)
    dv = dot_t0(prob_low, do)
    for n, part in enumerate((dk, dv)):
        for s in range(3):
            first = s * SEG
            dabove_ref[n, s] = part[first : first + EDGE].astype(BF16)
            dmid_ref[n, s] = part[first + EDGE : first + EDGE + tokens]
            dbelow_ref[n, s] = part[first + EDGE + tokens : first + USED].astype(BF16)
    bias_all[...] = dscore
    tail = jnp.zeros((COLS, SHIFTED - SEG), F32)
    for s in range(3):
        acc = None
        for i in range(ROWS):
            off = (ROWS - 1 - i) * COLS
            piece = bias_all[i * COLS : (i + 1) * COLS, s * SEG : (s + 1) * SEG]
            piece = jnp.concatenate([piece, tail], axis=1)
            if off:
                piece = pltpu.roll(piece, off, 1)
            acc = piece if acc is None else acc + piece
        table_ref[0, s] = acc


def attn_backward(queries, parts, above, mid, below, bias_rows, mask):
    tokens, width = queries.shape
    heads = width // HEAD_DIM
    groups = parts.shape[0]
    edge_spec = pl.BlockSpec((2, 3, EDGE, HEAD_DIM), lambda h: (0, 0, 0, h))
    mid_spec = pl.BlockSpec((2, 3, tokens, HEAD_DIM), lambda h: (0, 0, 0, h))
    edge_low = jax.ShapeDtypeStruct((2, 3, EDGE, width), BF16)
    return pl.pallas_call(
        attn_body,
        grid=(heads,),
        in_specs=[
            pl.BlockSpec((tokens, HEAD_DIM), lambda h: (0, h)),
            pl.BlockSpec((groups, tokens, HEAD_DIM), lambda h: (0, 0, h)),
            edge_spec,
            mid_spec,
            edge_spec,
            pl.BlockSpec((1, 2, SHIFTED), lambda h: (h, 0, 0)),
            pl.BlockSpec((ROWS, 3 * SEG), lambda h: (0, 0)),
        ],
        out_specs=[
            pl.BlockSpec((tokens, HEAD_DIM), lambda h: (0, h)),
            edge_spec,
            mid_spec,
            edge_spec,
            pl.BlockSpec((1, 3, COLS, SHIFTED), lambda h: (h, 0, 0, 0)),
        ],
        out_shape=[
            jax.ShapeDtypeStruct((tokens, width), BF16),
            edge_low,
            jax.ShapeDtypeStruct((2, 3, tokens, width), F32),
            edge_low,
            jax.ShapeDtypeStruct((heads, 3, COLS, SHIFTED), F32),
        ],
        scratch_shapes=[pltpu.VMEM((tokens, 3 * SEG), F32)],
        name="attn_backward",
    )(queries, parts, above, mid, below, bias_rows, mask)


def shift(value, axis, step, wrap):
    count = lax.axis_size(axis)
    pairs = [
        (i, (i + step) % count) for i in range(count) if wrap or 0 <= i + step < count
    ]
    return lax.ppermute(value, axis, pairs)


def make_mask(key_mask):
    lat_total, lon_total = key_mask.shape
    lat, lon = lax.axis_index(LAT), lax.axis_index(LON)
    rows = lax.broadcasted_iota(jnp.int32, key_mask.shape, 0)
    cols = lax.broadcasted_iota(jnp.int32, key_mask.shape, 1)
    valid = ((key_mask == 1) | ((rows % 4 == 0) & (cols % 4 == 0))).astype(F32)
    valid = jnp.pad(valid, ((REACH, SEG_ROWS - ROWS - REACH), (0, 0)))
    valid = jnp.concatenate([valid[:, -COLS:], valid, valid[:, :COLS]], axis=1)
    valid = lax.dynamic_slice(valid, (lat * ROWS, lon * COLS), (SEG_ROWS, 3 * COLS))
    valid = valid.reshape(SEG_ROWS, 3, COLS).transpose(1, 0, 2).reshape(1, 3 * SEG)
    row_of = (lax.broadcasted_iota(jnp.int32, (ROWS, 3 * SEG), 1) // COLS) % SEG_ROWS
    query = lat * ROWS + lax.broadcasted_iota(jnp.int32, (ROWS, 3 * SEG), 0)
    low = jnp.clip(query - REACH, 0, lat_total - WIN) - lat * ROWS + REACH
    allowed = (row_of >= low) & (row_of < low + WIN) & (valid > 0)
    return jnp.where(allowed, 0.0, NEG).astype(F32)


def spread_bias(table):
    heads, offsets, _ = table.shape
    above = ROWS - 1 - REACH
    padded = jnp.pad(
        table,
        ((0, 0), (above, SEG_ROWS + ROWS - offsets - above), (0, 2 * COLS - WIN)),
        constant_values=NEG,
    )
    padded = padded.reshape(heads, SEG_ROWS + ROWS, 2, COLS)
    return padded.transpose(0, 2, 1, 3).reshape(heads, 2, SHIFTED)


def gather_table(spread):
    heads = spread.shape[0]
    offsets = 2 * WIN - 1
    first_row = ROWS - 1 - REACH
    grid = spread.reshape(heads, 3, COLS, SEG_ROWS + ROWS, COLS)[:, :, :, first_row : first_row + offsets]
    pad_y = COLS + 1
    total = jnp.zeros((heads, offsets, WIN + 2 * pad_y), F32)
    for s in range(3):
        for j in range(COLS):
            first = COLS * (s - 1) - j + REACH + pad_y
            total = total + jnp.pad(
                grid[:, s, j], ((0, 0), (0, 0), (first, WIN + 2 * pad_y - COLS - first))
            )
    return total[:, :, pad_y : pad_y + WIN]


def pack_cols(value):
    return value.transpose(0, 2, 1, 3)


def local(queries, keys, values, attn_out, grad_out, w_out, bias_table, key_mask):
    lat_rows, lon_cols, width = queries.shape
    tokens = lat_rows * lon_cols
    feats_local = grad_out.shape[2]
    x_n, chan_n = (lax.axis_size(axis) for axis in ("x", "chan"))
    w_rows_local = w_out.shape[0]
    per_chan = feats_local // (2 * x_n * w_rows_local)
    feats = 2 * w_rows_local
    core, x = lax.axis_index("core"), lax.axis_index("x")
    swap = [(0, 1), (1, 0)]
    skip = COLS - REACH

    grad_t = grad_out.reshape(tokens, feats_local).T
    grad_t = grad_t.reshape(per_chan * 2, x_n, w_rows_local, tokens).transpose(1, 0, 2, 3)
    grad_t = grad_t.reshape(x_n, 1, per_chan * feats, tokens)
    grad_t = jnp.broadcast_to(grad_t, (x_n, chan_n, per_chan * feats, tokens))
    grad_t = grad_t.reshape(x_n * chan_n, per_chan * feats, tokens)
    grad_t, attn_out, w_out, keys, values = lax.optimization_barrier(
        (grad_t, attn_out, w_out, keys, values)
    )
    grad_feats = lax.all_to_all(grad_t, ("x", "chan"), 0, 0)
    grad_feats = grad_feats.reshape(x_n, chan_n, per_chan, feats, tokens)

    w_own = lax.all_gather(w_out, RING, axis=0).reshape(chan_n * feats, width)
    w_other = lax.ppermute(w_own, "core", swap)

    attn_rows = [attn_out.reshape(tokens, width)]
    attn_rows += [shift(attn_rows[0], "x", r, True) for r in range(1, x_n)]

    kv = jnp.stack([keys, values])
    from_left = shift(pack_cols(kv[:, :, skip:]), LON, 1, True)
    from_right = shift(pack_cols(kv[:, :, :REACH]), LON, -1, True)
    left = jnp.pad(pack_cols(from_left), ((0, 0), (0, 0), (skip, 0), (0, 0)))
    right = jnp.pad(pack_cols(from_right), ((0, 0), (0, 0), (0, skip), (0, 0)))
    mid = jnp.stack([left, kv, right], axis=1).reshape(2, 3, tokens, width)
    above = shift(mid[:, :, tokens - EDGE :], LAT, 1, False)
    below = shift(mid[:, :, :EDGE], LAT, -1, False)

    parts = grad_attn_parts(grad_feats, w_own, w_other, core.reshape(1))
    parts, grad_feats = lax.optimization_barrier((parts, grad_feats))
    parts = lax.all_to_all(parts, "x", 0, 0)
    wout_mine, wout_other = grad_wout_parts(grad_feats, attn_rows, jnp.stack([core, x]))
    wout_mine = wout_mine + lax.ppermute(wout_other, "core", swap).astype(F32)
    wout_parts = wout_mine.astype(BF16).reshape(chan_n * 2, w_rows_local, width)
    parts, wout_parts = lax.optimization_barrier((parts, wout_parts))
    wout_parts = lax.all_to_all(wout_parts, RING, 0, 0)
    dq, dabove, dmid, dbelow, spread = attn_backward(
        queries.reshape(tokens, width),
        parts,
        above,
        mid,
        below,
        spread_bias(bias_table),
        make_mask(key_mask),
    )
    from_below = shift(dabove, LAT, -1, False).astype(F32)
    from_above = shift(dbelow, LAT, 1, False).astype(F32)
    table = gather_table(spread)
    table = jnp.pad(table.reshape(-1), (0, -table.size % 128)).reshape(-1, 128)
    gap = tokens - EDGE
    folded = dmid + jnp.pad(from_above, ((0, 0), (0, 0), (0, gap), (0, 0)))
    folded = folded + jnp.pad(from_below, ((0, 0), (0, 0), (gap, 0), (0, 0)))
    folded = folded.reshape(2, 3, lat_rows, lon_cols, width)
    to_left = pack_cols(folded[:, 0, :, skip:].astype(BF16))
    to_right = pack_cols(folded[:, 2, :, :REACH].astype(BF16))
    wout_parts, table = lax.optimization_barrier((wout_parts, table))
    from_right = shift(to_left, LON, -1, True)
    from_left = shift(to_right, LON, 1, True)
    everyone = (*LAT, *LON)
    count = lax.axis_size(everyone)
    table = lax.all_to_all(jnp.broadcast_to(table[None], (count, *table.shape)), everyone, 0, 0)
    grad_table = jnp.sum(table, axis=0).reshape(-1)[: bias_table.size].reshape(bias_table.shape)
    total = folded[:, 1]
    total = total + jnp.pad(
        pack_cols(from_right).astype(F32), ((0, 0), (0, 0), (skip, 0), (0, 0))
    )
    total = total + jnp.pad(
        pack_cols(from_left).astype(F32), ((0, 0), (0, 0), (0, skip), (0, 0))
    )
    total = total.astype(BF16)
    grad_wout = jnp.sum(wout_parts.astype(F32), axis=0)
    return (
        dq.reshape(lat_rows, lon_cols, width),
        total[0],
        total[1],
        grad_wout,
        grad_table,
    )


def solution(mesh):
    lat_n, lon_n, chan_n = (mesh.shape[axis] for axis in ("lat", "lon", "chan"))
    split = jax.sharding.Mesh(
        mesh.devices.reshape(lat_n // 2, 2, 2, lon_n // 2, chan_n), (*LAT, *LON, "chan")
    )
    token_spec = P(LAT, LON, "chan")
    w_spec = P((*LAT, *LON), "chan")
    table_spec = P("chan", None, None)
    return jax.shard_map(
        local,
        mesh=split,
        in_specs=(token_spec,) * 5 + (w_spec, table_spec, P()),
        out_specs=(token_spec,) * 3 + (w_spec, table_spec),
        check_vma=False,
    )
```

```python
import jax
import jax.numpy as jnp
from jax import lax
from jax.experimental import pallas as pl
from jax.experimental.pallas import tpu as pltpu
from jax.sharding import PartitionSpec as P


HEAD_DIM = 128
WIN = 13
LON = ("zh", "x")
LAT = ("zl", "core")
RING = ("zh", "zl")
REACH = 6
NEG = -1e30
F32 = jnp.float32
BF16 = jnp.bfloat16
SEG_ROWS = 32
ROWS = 16
COLS = 8
EXT_ROWS = ROWS + 2 * REACH
SEG = SEG_ROWS * COLS
USED = EXT_ROWS * COLS
EDGE = REACH * COLS
SHIFTED = (SEG_ROWS + ROWS) * COLS


def dot_t0(a, b):
    return lax.dot_general(a, b, (((0,), (0,)), ((), ())), preferred_element_type=F32)


def dot_t1(a, b):
    return lax.dot_general(a, b, (((1,), (1,)), ((), ())), preferred_element_type=F32)


def grad_attn_body(core_ref, grad_ref, own_ref, other_ref, out_ref):
    core = core_ref[0]
    chans, rows = grad_ref.shape[1], grad_ref.shape[3] // 2
    total = None
    for w_ref, pick in ((own_ref, core), (other_ref, 1 - core)):
        grads = [grad_ref[0, c, pick] for c in range(chans)]
        grads = jnp.concatenate(
            [g[z * rows : (z + 1) * rows] for z in range(2) for g in grads], axis=0
        )
        part = dot_t0(grads, w_ref[...])
        total = part if total is None else total + part
    out_ref[0] = total.astype(BF16)


def grad_attn_parts(grad_feats, w_own, w_other, core):
    groups, chans, cores, feats, tokens = grad_feats.shape
    width = w_own.shape[1]
    w_spec = pl.BlockSpec(w_own.shape, lambda i, _: (0, 0))
    return pl.pallas_call(
        grad_attn_body,
        grid_spec=pltpu.PrefetchScalarGridSpec(
            num_scalar_prefetch=1,
            grid=(groups,),
            in_specs=[
                pl.BlockSpec((1, chans, cores, feats, tokens), lambda i, _: (i, 0, 0, 0, 0)),
                w_spec,
                w_spec,
            ],
            out_specs=pl.BlockSpec((1, tokens, width), lambda i, _: (i, 0, 0)),
        ),
        out_shape=jax.ShapeDtypeStruct((groups, tokens, width), BF16),
        name="grad_attn_parts",
    )(core, grad_feats, w_own, w_other)


def grad_wout_body(place_ref, grad_ref, *refs):
    attn_refs, (mine_ref, other_ref) = refs[:-2], refs[-2:]
    groups = grad_ref.shape[0]
    core, x = place_ref[0], place_ref[1]
    attn = jnp.concatenate([ref[...] for ref in attn_refs], axis=0)
    for out_ref, pick in ((mine_ref, core), (other_ref, 1 - core)):
        grads = jnp.concatenate(
            [grad_ref[(x + groups - r) % groups, 0, pick] for r in range(groups)], axis=1
        )
        part = jnp.dot(grads, attn, preferred_element_type=F32)
        rows = out_ref.shape[2]
        for z in range(2):
            out_ref[z, 0] = part[z * rows : (z + 1) * rows].astype(out_ref.dtype)


def grad_wout_parts(grad_feats, attn_rows, place):
    groups, chans, cores, feats, tokens = grad_feats.shape
    width = attn_rows[0].shape[1]
    out_spec = pl.BlockSpec((2, 1, feats // 2, width), lambda c, _: (0, c, 0, 0))
    attn_spec = pl.BlockSpec((tokens, width), lambda c, _: (0, 0))
    return pl.pallas_call(
        grad_wout_body,
        grid_spec=pltpu.PrefetchScalarGridSpec(
            num_scalar_prefetch=1,
            grid=(chans,),
            in_specs=[
                pl.BlockSpec((groups, 1, cores, feats, tokens), lambda c, _: (0, c, 0, 0, 0)),
            ]
            + [attn_spec] * groups,
            out_specs=[out_spec, out_spec],
        ),
        out_shape=[
            jax.ShapeDtypeStruct((2, chans, feats // 2, width), F32),
            jax.ShapeDtypeStruct((2, chans, feats // 2, width), BF16),
        ],
        name="grad_wout_parts",
    )(place, grad_feats, *attn_rows)


def spread_rows(halves):
    shape = (COLS, SHIFTED)
    low = jnp.broadcast_to(halves[0:1], shape)
    high = jnp.broadcast_to(halves[1:2], shape)
    lane = lax.broadcasted_iota(jnp.int32, shape, 1) % COLS
    rel = lane - lax.broadcasted_iota(jnp.int32, shape, 0) - (COLS - REACH)

    def turn(value, first):
        if first < 0:
            value = pltpu.roll(value, first % SHIFTED, 1)
        return pltpu.roll(value, max(first, 0), 1, stride=1, stride_axis=0)

    skip = COLS - REACH
    none = jnp.full(shape, NEG, F32)
    return (
        jnp.where(rel >= 0, turn(low, skip), none),
        jnp.where(rel >= 0, turn(high, skip), jnp.where(rel >= -COLS, turn(low, skip - COLS), none)),
        jnp.where(
            rel >= 0,
            none,
            jnp.where(rel >= -COLS, turn(high, skip - COLS), turn(low, skip - 2 * COLS)),
        ),
    )


def attn_body(q_ref, part_ref, above_ref, mid_ref, below_ref, bias_ref, mask_ref,
              dq_ref, dabove_ref, dmid_ref, dbelow_ref, table_ref, bias_all):
    scale = HEAD_DIM ** (-0.5)
    tokens = ROWS * COLS
    spread = spread_rows(bias_ref[0])
    for i in range(ROWS):
        off = (ROWS - 1 - i) * COLS
        for s in range(3):
            row = spread[s]
            if off:
                row = pltpu.roll(row, SHIFTED - off, 1)
            row = row[:, :SEG] + mask_ref[i : i + 1, s * SEG : (s + 1) * SEG]
            bias_all[i * COLS : (i + 1) * COLS, s * SEG : (s + 1) * SEG] = row
    q = q_ref[...]
    do_sum = part_ref[0].astype(F32)
    for g in range(1, part_ref.shape[0]):
        do_sum = do_sum + part_ref[g].astype(F32)
    do = do_sum.astype(BF16)
    fill = jnp.zeros((SEG - USED, HEAD_DIM), BF16)
    k, v = (
        jnp.concatenate(
            [
                piece
                for s in range(3)
                for piece in (above_ref[n, s], mid_ref[n, s], below_ref[n, s], fill)
            ],
            axis=0,
        )
        for n in range(2)
    )
    scores = dot_t1(q, k) * scale + bias_all[...]
    row_max = jnp.max(scores, axis=1, keepdims=True)
    weights = jnp.exp(scores - row_max)
    probs = weights * (1.0 / jnp.sum(weights, axis=1, keepdims=True))
    grad_probs = dot_t1(do, v)
    delta = jnp.sum(probs * grad_probs, axis=1, keepdims=True)
    dscore = probs * (grad_probs - delta)
    dscore_low = dscore.astype(BF16)
    prob_low = probs.astype(BF16)
    dq_ref[...] = (scale * jnp.dot(dscore_low, k, preferred_element_type=F32)).astype(BF16)
    dk = scale * dot_t0(dscore_low, q)
    dv = dot_t0(prob_low, do)
    for n, part in enumerate((dk, dv)):
        for s in range(3):
            first = s * SEG
            dabove_ref[n, s] = part[first : first + EDGE].astype(BF16)
            dmid_ref[n, s] = part[first + EDGE : first + EDGE + tokens]
            dbelow_ref[n, s] = part[first + EDGE + tokens : first + USED].astype(BF16)
    bias_all[...] = dscore
    tail = jnp.zeros((COLS, SHIFTED - SEG), F32)
    for s in range(3):
        acc = None
        for i in range(ROWS):
            off = (ROWS - 1 - i) * COLS
            piece = bias_all[i * COLS : (i + 1) * COLS, s * SEG : (s + 1) * SEG]
            piece = jnp.concatenate([piece, tail], axis=1)
            if off:
                piece = pltpu.roll(piece, off, 1)
            acc = piece if acc is None else acc + piece
        table_ref[0, s] = acc


def attn_backward(queries, parts, above, mid, below, bias_rows, mask):
    tokens, width = queries.shape
    heads = width // HEAD_DIM
    groups = parts.shape[0]
    edge_spec = pl.BlockSpec((2, 3, EDGE, HEAD_DIM), lambda h: (0, 0, 0, h))
    mid_spec = pl.BlockSpec((2, 3, tokens, HEAD_DIM), lambda h: (0, 0, 0, h))
    edge_low = jax.ShapeDtypeStruct((2, 3, EDGE, width), BF16)
    return pl.pallas_call(
        attn_body,
        grid=(heads,),
        in_specs=[
            pl.BlockSpec((tokens, HEAD_DIM), lambda h: (0, h)),
            pl.BlockSpec((groups, tokens, HEAD_DIM), lambda h: (0, 0, h)),
            edge_spec,
            mid_spec,
            edge_spec,
            pl.BlockSpec((1, 2, SHIFTED), lambda h: (h, 0, 0)),
            pl.BlockSpec((ROWS, 3 * SEG), lambda h: (0, 0)),
        ],
        out_specs=[
            pl.BlockSpec((tokens, HEAD_DIM), lambda h: (0, h)),
            edge_spec,
            mid_spec,
            edge_spec,
            pl.BlockSpec((1, 3, COLS, SHIFTED), lambda h: (h, 0, 0, 0)),
        ],
        out_shape=[
            jax.ShapeDtypeStruct((tokens, width), BF16),
            edge_low,
            jax.ShapeDtypeStruct((2, 3, tokens, width), F32),
            edge_low,
            jax.ShapeDtypeStruct((heads, 3, COLS, SHIFTED), F32),
        ],
        scratch_shapes=[pltpu.VMEM((tokens, 3 * SEG), F32)],
        name="attn_backward",
    )(queries, parts, above, mid, below, bias_rows, mask)


def shift(value, axis, step, wrap):
    count = lax.axis_size(axis)
    pairs = [
        (i, (i + step) % count) for i in range(count) if wrap or 0 <= i + step < count
    ]
    return lax.ppermute(value, axis, pairs)


def make_mask(key_mask):
    lat_total, _ = key_mask.shape
    lat, lon = lax.axis_index(LAT), lax.axis_index(LON)
    rows = lax.broadcasted_iota(jnp.int32, key_mask.shape, 0)
    cols = lax.broadcasted_iota(jnp.int32, key_mask.shape, 1)
    valid = ((key_mask == 1) | ((rows % 4 == 0) & (cols % 4 == 0))).astype(F32)
    valid = jnp.pad(valid, ((REACH, SEG_ROWS - ROWS - REACH), (0, 0)))
    valid = jnp.concatenate([valid[:, -COLS:], valid, valid[:, :COLS]], axis=1)
    valid = lax.dynamic_slice(valid, (lat * ROWS, lon * COLS), (SEG_ROWS, 3 * COLS))
    valid = valid.reshape(SEG_ROWS, 3, COLS).transpose(1, 0, 2).reshape(1, 3 * SEG)
    row_of = (lax.broadcasted_iota(jnp.int32, (ROWS, 3 * SEG), 1) // COLS) % SEG_ROWS
    query = lat * ROWS + lax.broadcasted_iota(jnp.int32, (ROWS, 3 * SEG), 0)
    low = jnp.clip(query - REACH, 0, lat_total - WIN) - lat * ROWS + REACH
    allowed = (row_of >= low) & (row_of < low + WIN) & (valid > 0)
    return jnp.where(allowed, 0.0, NEG).astype(F32)


def spread_bias(table):
    heads, offsets, _ = table.shape
    above = ROWS - 1 - REACH
    padded = jnp.pad(
        table,
        ((0, 0), (above, SEG_ROWS + ROWS - offsets - above), (0, 2 * COLS - WIN)),
        constant_values=NEG,
    )
    padded = padded.reshape(heads, SEG_ROWS + ROWS, 2, COLS)
    return padded.transpose(0, 2, 1, 3).reshape(heads, 2, SHIFTED)


def gather_table(spread):
    heads = spread.shape[0]
    offsets = 2 * WIN - 1
    first_row = ROWS - 1 - REACH
    grid = spread.reshape(heads, 3, COLS, SEG_ROWS + ROWS, COLS)[:, :, :, first_row : first_row + offsets]
    pad_y = COLS + 1
    total = jnp.zeros((heads, offsets, WIN + 2 * pad_y), F32)
    for s in range(3):
        for j in range(COLS):
            first = COLS * (s - 1) - j + REACH + pad_y
            total = total + jnp.pad(
                grid[:, s, j], ((0, 0), (0, 0), (first, WIN + 2 * pad_y - COLS - first))
            )
    return total[:, :, pad_y : pad_y + WIN]


def pack_cols(value):
    return value.transpose(0, 2, 1, 3)


def local(queries, keys, values, attn_out, grad_out, w_out, bias_table, key_mask):
    lat_rows, lon_cols, width = queries.shape
    tokens = lat_rows * lon_cols
    feats_local = grad_out.shape[2]
    x_n, chan_n = (lax.axis_size(axis) for axis in ("x", "chan"))
    w_rows_local = w_out.shape[0]
    per_chan = feats_local // (2 * x_n * w_rows_local)
    feats = 2 * w_rows_local
    core, x = lax.axis_index("core"), lax.axis_index("x")
    swap = [(0, 1), (1, 0)]
    skip = COLS - REACH

    grad_t = grad_out.reshape(tokens, feats_local).T
    grad_t = grad_t.reshape(per_chan * 2, x_n, w_rows_local, tokens).transpose(1, 0, 2, 3)
    grad_t = grad_t.reshape(x_n, 1, per_chan * feats, tokens)
    grad_t = jnp.broadcast_to(grad_t, (x_n, chan_n, per_chan * feats, tokens))
    grad_t = grad_t.reshape(x_n * chan_n, per_chan * feats, tokens)
    grad_t, attn_out, w_out, keys, values = lax.optimization_barrier(
        (grad_t, attn_out, w_out, keys, values)
    )
    grad_feats = lax.all_to_all(grad_t, ("x", "chan"), 0, 0)
    grad_feats = grad_feats.reshape(x_n, chan_n, per_chan, feats, tokens)

    w_own = lax.all_gather(w_out, RING, axis=0)
    w_own = w_own.reshape(chan_n * feats, width)
    w_other = lax.ppermute(w_own, "core", swap)

    attn_rows = [attn_out.reshape(tokens, width)]
    attn_rows += [shift(attn_rows[0], "x", r, True) for r in range(1, x_n)]

    kv = jnp.stack([keys, values])
    from_left = shift(pack_cols(kv[:, :, skip:]), LON, 1, True)
    from_right = shift(pack_cols(kv[:, :, :REACH]), LON, -1, True)
    left = jnp.pad(pack_cols(from_left), ((0, 0), (0, 0), (skip, 0), (0, 0)))
    right = jnp.pad(pack_cols(from_right), ((0, 0), (0, 0), (0, skip), (0, 0)))
    mid = jnp.stack([left, kv, right], axis=1).reshape(2, 3, tokens, width)
    above = shift(mid[:, :, tokens - EDGE :], LAT, 1, False)
    below = shift(mid[:, :, :EDGE], LAT, -1, False)

    parts = grad_attn_parts(grad_feats, w_own, w_other, core.reshape(1))
    parts, grad_feats = lax.optimization_barrier((parts, grad_feats))
    parts = lax.all_to_all(parts, "x", 0, 0)
    wout_mine, wout_other = grad_wout_parts(grad_feats, attn_rows, jnp.stack([core, x]))
    wout_other = lax.ppermute(wout_other, "core", swap)
    wout_mine = wout_mine + wout_other.astype(F32)
    wout_parts = wout_mine.astype(BF16).reshape(chan_n * 2, w_rows_local, width)
    parts, wout_parts = lax.optimization_barrier((parts, wout_parts))
    wout_parts = lax.all_to_all(wout_parts, RING, 0, 0)
    dq, dabove, dmid, dbelow, spread = attn_backward(
        queries.reshape(tokens, width),
        parts,
        above,
        mid,
        below,
        spread_bias(bias_table),
        make_mask(key_mask),
    )
    from_below = shift(dabove, LAT, -1, False).astype(F32)
    from_above = shift(dbelow, LAT, 1, False).astype(F32)
    table = gather_table(spread)
    table = jnp.pad(table.reshape(-1), (0, -table.size % 128)).reshape(-1, 128)
    gap = tokens - EDGE
    folded = dmid + jnp.pad(from_above, ((0, 0), (0, 0), (0, gap), (0, 0)))
    folded = folded + jnp.pad(from_below, ((0, 0), (0, 0), (gap, 0), (0, 0)))
    folded = folded.reshape(2, 3, lat_rows, lon_cols, width)
    to_left = pack_cols(folded[:, 0, :, skip:].astype(BF16))
    to_right = pack_cols(folded[:, 2, :, :REACH].astype(BF16))
    wout_parts, table = lax.optimization_barrier((wout_parts, table))
    from_right = shift(to_left, LON, -1, True)
    from_left = shift(to_right, LON, 1, True)
    everyone = (*LAT, *LON)
    count = lax.axis_size(everyone)
    table = jnp.broadcast_to(table[None], (count, *table.shape))
    table = lax.all_to_all(table, everyone, 0, 0)
    grad_table = jnp.sum(table, axis=0).reshape(-1)[: bias_table.size].reshape(bias_table.shape)
    total = folded[:, 1]
    total = total + jnp.pad(
        pack_cols(from_right).astype(F32), ((0, 0), (0, 0), (skip, 0), (0, 0))
    )
    total = total + jnp.pad(
        pack_cols(from_left).astype(F32), ((0, 0), (0, 0), (0, skip), (0, 0))
    )
    total = total.astype(BF16)
    grad_wout = jnp.sum(wout_parts.astype(F32), axis=0)
    return (
        dq.reshape(lat_rows, lon_cols, width),
        total[0],
        total[1],
        grad_wout,
        grad_table,
    )


def solution(mesh):
    lat_n, lon_n, chan_n = (mesh.shape[axis] for axis in ("lat", "lon", "chan"))
    split = jax.sharding.Mesh(
        mesh.devices.reshape(lat_n // 2, 2, 2, lon_n // 2, chan_n), (*LAT, *LON, "chan")
    )
    token_spec = P(LAT, LON, "chan")
    w_spec = P((*LAT, *LON), "chan")
    table_spec = P("chan", None, None)
    return jax.shard_map(
        local,
        mesh=split,
        in_specs=(token_spec,) * 5 + (w_spec, table_spec, P()),
        out_specs=(token_spec,) * 3 + (w_spec, table_spec),
        check_vma=False,
    )
```
